32 devices in a mesh: dp: 16 (over z, x, core), fac: 2 (over y).
Axes of the slice: x: 2, y: 2, z: 4, core: 2. Of those that a mesh axis runs over, the one named last changes fastest.
Arguments:
- occupations: int32 [32, 256], P('dp'), may hold values from 0 to 1, as said below
- stream: bfloat16 [8192, 2048], P('dp', 'fac'), may hold values from -6 to 6
- norm_gain: float32 [2048], replicated, may hold values from 0.1 to 1.9
- probs: bfloat16 [32, 16, 256, 256], P('dp', 'fac'), may hold values from 0 to 1, as said below
- w_out: bfloat16 [2048, 2048], P('fac', 'dp'), may hold values from -0.125 to 0.125
- cotangent: bfloat16 [8192, 2048], P('dp', 'fac'), may hold values from -6 to 6
Outputs:
- update: float32 [2048, 2048], P('dp', 'fac')
The draws below stay inside these ranges and needn't reach their ends.
Inputs may be any that keep to these rules, and one draw needn't show every extreme that they name: `occupations`: each sample holds exactly 48 ones. `probs`: within each sample and head, entries with the key after the query are zero and each row sums to one up to bfloat16 rounding.
All inputs are finite; a program needn't handle non-finite values.
Results may differ from the reference program's by a relative error of at most 0.0051.
Values may be sent and summed in bfloat16 or wider, within the bound.
No kernel may reach another device: no remote copies, remote signals or barrier semaphores. Data moves between devices by JAX's collectives and lax.ppermute only.
A program may use at most 128 MiB of HBM per device.

```python
import math
import jax
import jax.numpy as jnp
from jax import lax

D = 2048
HEADS = 16
ORBS = 256
NE = 48
ITERS = 2
SAMPLES = 32
TOKENS = 8192


def shuffled(one_key):
    return jax.random.permutation(one_key, ORBS)


def draw_occupations(key, part):
    sample_keys = jax.random.split(jax.random.fold_in(key, 7), SAMPLES)
    orders = jax.vmap(shuffled)(sample_keys)
    return (orders < NE).astype(jnp.int32)


def draw_probs(key, part):
    noise_key = jax.random.fold_in(key, 11)
    rate_key = jax.random.fold_in(key, 12)
    shape = (SAMPLES, HEADS, ORBS, ORBS)
    noise = 1.5 * jax.random.normal(noise_key, shape, jnp.float32)
    rates = jnp.exp(jax.random.uniform(rate_key, (1, HEADS, 1, 1), jnp.float32, math.log(0.5), math.log(8.0))) / ORBS
    query_index = lax.broadcasted_iota(jnp.int32, (ORBS, ORBS), 0)
    key_index = lax.broadcasted_iota(jnp.int32, (ORBS, ORBS), 1)
    distance = (query_index - key_index).astype(jnp.float32)
    scores = noise - rates * distance
    scores = jnp.where(key_index <= query_index, scores, -1e+30)
    scores = scores - jnp.max(scores, axis=-1, keepdims=True)
    weights = jnp.exp(scores)
    return (weights / jnp.sum(weights, axis=-1, keepdims=True)).astype(jnp.bfloat16)


def block_levels(stream_key, extent, pieces, low, largest):
    factor_of, own = 1.0, jax.random.fold_in(stream_key, 6)
    for dim, parts in pieces:
        heights = jnp.exp(jax.random.uniform(jax.random.fold_in(own, dim), (parts,), jnp.float32, low / len(pieces), largest / len(pieces)))
        factor_of = factor_of * jnp.repeat(heights, extent[dim] // parts).reshape([-1 if axis == dim else 1 for axis in range(len(extent))])
    return factor_of


def gaussian(own_key, shape, spread, limit, cuts=(), held_as=jnp.bfloat16):
    gain = block_levels(own_key, shape, cuts, -0.22, 0.18) if cuts else 1.0
    values = jax.random.normal(own_key, shape, jnp.float32) * spread * gain
    return jnp.minimum(jnp.maximum(values, -limit), limit).astype(held_as)


def setup_inputs(seed: int = 0) -> dict:
    seeds = jax.random.split(jax.random.key(seed), 7)
    occupations = draw_occupations(jax.random.fold_in(seeds[6], 71), 0)
    stream = gaussian(seeds[1], (TOKENS, D), 1.0, 6.0, ((0, 16), (1, 2)))
    norm_gain = jnp.clip(1.0 + 0.18 * jax.random.normal(seeds[2], (D,), jnp.float32), 0.1, 1.9)
    probs = draw_probs(jax.random.fold_in(seeds[6], 71), 0)
    w_out = gaussian(seeds[4], (D, D), D ** -0.5, 0.125, ((0, 2), (1, 16)))
    cotangent = gaussian(seeds[5], (TOKENS, D), 1.0, 6.0, ((0, 16), (1, 2)))
    return {"occupations": occupations, "stream": stream, "norm_gain": norm_gain, "probs": probs, "w_out": w_out, "cotangent": cotangent}


damping = 0.1
epsilon = 1e-06
highest = lax.Precision.HIGHEST

def keep_mask(occupations):
    occupied = occupations.astype(jnp.int32)
    before = jnp.cumsum(occupied, axis=1).astype(jnp.int32) - occupied
    position = lax.broadcasted_iota(jnp.int32, occupied.shape, 1)
    forced = (before == NE) | (position - before == ORBS - NE)
    return 1 - forced.astype(jnp.int32)

def newton_schulz(factor):
    identity = jnp.eye(factor.shape[0], dtype=jnp.float32)
    alpha = 1.0 / jnp.sqrt(jnp.sum(factor * factor))
    iterate = 2.0 * alpha * identity - alpha * alpha * factor
    for iteration in range(ITERS - 1):
        product = jnp.dot(factor, iterate, precision=highest)
        iterate = 2.0 * iterate - jnp.dot(iterate, product, precision=highest)
    return iterate

def one_sample(inputs):
    weights, grads = inputs
    return jnp.einsum('hij,ihe->jhe', weights.astype(jnp.float32), grads.astype(jnp.float32))

def reference(occupations, stream, norm_gain, probs, w_out, cotangent):
    values = stream.astype(jnp.float32)
    mean_square = lax.optimization_barrier(jnp.mean(values * values, axis=1, keepdims=True))
    normed = (values * lax.rsqrt(mean_square + epsilon) * norm_gain).astype(jnp.bfloat16)
    keep = keep_mask(occupations).reshape(TOKENS, 1).astype(jnp.bfloat16)
    upstream = cotangent * keep
    out_grad = jnp.dot(upstream, w_out.T, preferred_element_type=jnp.float32).astype(jnp.bfloat16)
    per_head = out_grad.reshape(SAMPLES, ORBS, HEADS, D // HEADS)
    value_grad = lax.map(one_sample, (probs, per_head)).reshape(TOKENS, D).astype(jnp.bfloat16)
    scale = 1.0 / TOKENS
    identity = jnp.eye(D, dtype=jnp.float32)
    a_fac = jnp.dot(normed.T, normed, preferred_element_type=jnp.float32) * scale + damping * identity
    g_fac = jnp.dot(value_grad.T, value_grad, preferred_element_type=jnp.float32) * scale + damping * identity
    grad = jnp.dot(normed.T, value_grad, preferred_element_type=jnp.float32) * scale
    inv_a = newton_schulz(a_fac)
    inv_g = newton_schulz(g_fac)
    pre = jnp.dot(jnp.dot(inv_a, grad, precision=highest), inv_g, precision=highest)
    inner_sum = jnp.sum(grad * pre)
    return pre * (D / jnp.sqrt(inner_sum + epsilon))
```

```python
import functools

import jax
import jax.numpy as jnp
from jax import lax
from jax.experimental import pallas as pl
from jax.experimental.pallas import tpu as pltpu
from jax.sharding import PartitionSpec as P

ORBS = 256
NE = 48


damping = 0.1
epsilon = 1e-06
f32 = jnp.float32
bf16 = jnp.bfloat16
contract_first = (((0,), (0,)), ((), ()))


def keep_mask(occupations):
    before = jnp.cumsum(occupations, axis=1) - occupations
    position = lax.broadcasted_iota(jnp.int32, occupations.shape, 1)
    forced = (before == NE) | (position - before == ORBS - NE)
    return 1 - forced.astype(jnp.int32)


def grid_of(count):
    core = 2 if count % 2 == 0 else 1
    chips = count // core
    inner = 1
    while inner * inner * 4 <= chips:
        inner *= 2
    return chips // inner, inner, core


def swap(value, axis, step):
    size = lax.axis_size(axis)
    return lax.ppermute(value, axis, [(i, i ^ step) for i in range(size)])


def collect(value, axis, count, stride):
    return [value] + [swap(value, axis, k * stride) for k in range(1, count)]


def in_order(pieces, own, axis):
    if len(pieces) == 2:
        first, second = pieces
        lower = own == 0
        return jnp.concatenate(
            [jnp.where(lower, first, second), jnp.where(lower, second, first)], axis
        )
    width = pieces[0].shape[axis]
    shape = list(pieces[0].shape)
    shape[axis] = width * len(pieces)
    whole = jnp.zeros(shape, pieces[0].dtype)
    for k, piece in enumerate(pieces):
        whole = lax.dynamic_update_slice_in_dim(whole, piece, (own ^ k) * width, axis)
    return whole


def dot(left, right):
    return jnp.dot(left, right, preferred_element_type=f32)


def load_factor(own, piece_refs, firsts, factor, sem, rows):
    copies = []
    for ref, codes in zip(piece_refs, firsts):
        for n, code in enumerate(codes):
            place = pl.multiple_of((own ^ code) * rows, rows)
            copies.append(
                pltpu.make_async_copy(ref.at[pl.ds(n * rows, rows)], factor.at[pl.ds(place, rows)], sem)
            )
    for copy in copies:
        copy.start()
    for copy in copies:
        copy.wait()


def inverse_times(panel, factor, columns=None):
    size = factor.shape[0]
    step = min(256, size)
    total = jnp.zeros((8, size), f32)
    for r in range(0, size, step):
        part = factor[r : r + step, :].astype(f32)
        total = total + jnp.sum((part * part).reshape(step // 8, 8, size), axis=0)
    alpha = lax.rsqrt(jnp.sum(total, keepdims=True))
    first = 2.0 * alpha * panel - alpha * alpha * dot(panel.astype(bf16), factor[...])
    turned = dot(first.astype(bf16), factor[...])
    return 2.0 * first - (2.0 * alpha * turned - alpha * alpha * dot(turned.astype(bf16), factor[...]))


def left_kernel(firsts, rows, own_ref, panel_ref, *refs):
    piece_refs, (out_ref, factor, sem) = refs[: len(firsts)], refs[len(firsts) :]
    load_factor(own_ref[0], piece_refs, firsts, factor, sem, rows)
    result = inverse_times(panel_ref[...], factor).astype(bf16)
    width = out_ref.shape[2]
    for n in range(out_ref.shape[0]):
        out_ref[n] = result[:, n * width : (n + 1) * width]


def gathered_rows(own, blocks_ref, turned):
    count, rows, _ = blocks_ref.shape
    for n in range(count):
        turned[n * rows : (n + 1) * rows, :] = blocks_ref[own ^ n].astype(f32)
    return turned[...].T


def middle_kernel(firsts, rows, own_ref, blocks_ref, *refs):
    piece_refs, (out_ref, factor, turned, sem) = refs[: len(firsts)], refs[len(firsts) :]
    own = own_ref[0]
    load_factor(own, piece_refs, firsts, factor, sem, rows)
    result = inverse_times(gathered_rows(own, blocks_ref, turned), factor)
    turned[...] = result.T
    for n in range(out_ref.shape[0]):
        place = pl.multiple_of((own ^ n) * rows, rows)
        out_ref[n] = turned[pl.ds(place, rows), :]


def right_kernel(firsts, rows, own_ref, blocks_ref, *refs):
    piece_refs, (out_ref, factor, turned, sem) = refs[: len(firsts)], refs[len(firsts) :]
    own = own_ref[0]
    load_factor(own, piece_refs, firsts, factor, sem, rows)
    out_ref[...] = inverse_times(gathered_rows(own, blocks_ref, turned), factor)


def apply_call(kernel, name, own, panel, pieces, firsts, rows, out_shape, scratch):
    size = pieces[0].shape[1]
    vmem = pl.BlockSpec(memory_space=pltpu.VMEM)
    return pl.pallas_call(
        functools.partial(kernel, firsts, rows),
        name=name,
        in_specs=[pl.BlockSpec(memory_space=pltpu.SMEM), vmem]
        + [pl.BlockSpec(memory_space=pl.ANY)] * len(pieces),
        out_specs=vmem,
        out_shape=out_shape,
        scratch_shapes=[pltpu.VMEM((size, size), bf16)] + scratch + [pltpu.SemaphoreType.DMA],
        compiler_params=pltpu.CompilerParams(vmem_limit_bytes=56 * 1024 * 1024),
    )(own, panel, *pieces)


def per_device(occupations, stream, norm_gain, probs, w_out, cotangent):
    width = norm_gain.shape[0]
    samples = occupations.shape[0]
    tokens = samples * ORBS
    data_count = lax.axis_size("dp")
    fac_count = lax.axis_size("fac")
    outer, inner, cores = grid_of(data_count)
    data_index = lax.axis_index("dp")
    fac_index = lax.axis_index("fac")
    core_index = data_index % cores
    inner_index = data_index // cores % inner
    outer_index = data_index // (cores * inner)
    inner_step = cores
    outer_step = cores * inner
    block_cols = width // fac_count
    scale = 1.0 / (tokens * data_count)
    quarter = width // (fac_count * cores)
    slab = quarter // inner
    panel = slab // outer
    own = ((fac_index * cores + core_index) * inner + inner_index) * outer + outer_index
    own_operand = own.astype(jnp.int32).reshape(1)

    cotangent_whole = in_order(collect(cotangent, "fac", fac_count, 1), fac_index, 1)
    weights = jnp.stack(collect(w_out, "dp", outer, outer_step))
    weights = jnp.stack(collect(weights, "dp", inner, inner_step))
    weights = jnp.stack(collect(weights, "dp", cores, 1))
    stream_whole = in_order(collect(stream, "fac", fac_count, 1), fac_index, 1)
    w_whole = jnp.zeros((w_out.shape[0], width), bf16)
    for c in range(cores):
        for x in range(inner):
            for z in range(outer):
                place = (
                    (outer_index ^ z) * inner + (inner_index ^ x)
                ) * cores + (core_index ^ c)
                w_whole = lax.dynamic_update_slice(
                    w_whole, weights[c, x, z], (0, place * w_out.shape[1])
                )

    values = stream_whole.astype(f32)
    mean_square = jnp.mean(values * values, axis=1, keepdims=True)
    normed = (values * lax.rsqrt(mean_square + epsilon) * norm_gain).astype(bf16)
    keep = keep_mask(occupations).reshape(tokens, 1).astype(bf16)
    upstream = cotangent_whole * keep
    out_grad = lax.dot_general(
        upstream, w_whole, (((1,), (1,)), ((), ())), preferred_element_type=f32
    ).astype(bf16)
    local_heads = probs.shape[1]
    head_width = block_cols // local_heads
    per_head = out_grad.reshape(samples, ORBS, local_heads, head_width)
    value_local = jnp.einsum("shij,sihe->sjhe", probs, per_head, preferred_element_type=f32)
    value_local = value_local.reshape(tokens, block_cols).astype(bf16)
    value_whole = in_order(collect(value_local, "fac", fac_count, 1), fac_index, 1)
    normed = jnp.concatenate(collect(normed, "dp", cores, 1), axis=0)
    value = jnp.concatenate(collect(value_whole, "dp", cores, 1), axis=0)

    start = (fac_index * cores + core_index) * quarter

    def summed(left, right):
        parts = []
        for k in range(inner):
            rows = lax.dynamic_slice_in_dim(left, start + (inner_index ^ k) * slab, slab, 1)
            parts.append(
                lax.dot_general(rows, right, contract_first, preferred_element_type=f32) * scale
            )
        total = parts[0]
        for k in range(1, inner):
            total = total + swap(parts[k].astype(bf16), "dp", k * inner_step).astype(f32)
        total = total.reshape(outer, panel, width)
        pieces = [
            lax.dynamic_index_in_dim(total, outer_index ^ k, 0, keepdims=False) for k in range(outer)
        ]
        result = pieces[0]
        for k in range(1, outer):
            result = result + swap(pieces[k].astype(bf16), "dp", k * outer_step).astype(f32)
        return result

    row_ids = own * panel + lax.broadcasted_iota(jnp.int32, (panel, width), 0)
    col_ids = lax.broadcasted_iota(jnp.int32, (panel, width), 1)
    damp = damping * (row_ids == col_ids).astype(f32)

    def panels_of(block):
        pieces = collect(block, "dp", outer, outer_step)
        group = jnp.concatenate(pieces, axis=0)
        codes = list(range(outer))
        pieces = collect(group, "dp", inner, inner_step)
        group = jnp.concatenate(pieces, axis=0)
        codes = [code + outer * k for k in range(inner) for code in codes]
        pieces = collect(group, "fac", fac_count, 1)
        group = jnp.concatenate(pieces, axis=0)
        codes = [code + outer * inner * cores * k for k in range(fac_count) for code in codes]
        pieces = collect(group, "dp", cores, 1)
        return pieces, [[code + outer * inner * k for code in codes] for k in range(cores)]

    a_block = (summed(normed, normed) + damp).astype(bf16)
    a_pieces, firsts = panels_of(a_block)
    g_block = (summed(value, value) + damp).astype(bf16)
    grad_cols = summed(value, normed)
    g_pieces, _ = panels_of(g_block)

    out_rows = width // data_count

    def exchange(blocks):
        blocks = blocks.reshape(outer, inner, cores, panel, out_rows)
        at = lambda part, index, axis: lax.dynamic_index_in_dim(part, index, axis, keepdims=False)
        blocks = jnp.stack(
            [at(blocks, core_index, 2)]
            + [swap(at(blocks, core_index ^ k, 2), "dp", k) for k in range(1, cores)]
        )
        blocks = jnp.stack(
            [at(blocks, inner_index, 2)]
            + [swap(at(blocks, inner_index ^ k, 2), "dp", k * inner_step) for k in range(1, inner)],
            axis=1,
        )
        blocks = jnp.stack(
            [at(blocks, outer_index, 2)]
            + [swap(at(blocks, outer_index ^ k, 2), "dp", k * outer_step) for k in range(1, outer)],
            axis=2,
        )
        blocks = blocks.reshape(cores * inner * outer, panel, out_rows)
        return jnp.concatenate(collect(blocks, "fac", fac_count, 1), axis=0)

    grad_blocks = jnp.transpose(
        grad_cols.astype(bf16).reshape(panel, data_count, out_rows), (1, 0, 2)
    )
    grad_rows = exchange(grad_blocks)
    left = apply_call(
        left_kernel,
        "left",
        own_operand,
        grad_cols,
        a_pieces,
        firsts,
        panel,
        jax.ShapeDtypeStruct((data_count, panel, out_rows), bf16),
        [],
    )
    panels = data_count * fac_count
    turned = pltpu.VMEM((width, out_rows), f32)
    right_grad = apply_call(
        middle_kernel,
        "middle",
        own_operand,
        grad_rows,
        g_pieces,
        firsts,
        panel,
        jax.ShapeDtypeStruct((panels, panel, out_rows), f32),
        [turned],
    )
    left_rows = exchange(left)
    inner_sum = jnp.sum(left_rows[:data_count].astype(f32) * right_grad[:data_count]).reshape(1, 1)
    for axis, size in (("fac", fac_count), ("dp", data_count)):
        step = 1
        while step < size:
            inner_sum = inner_sum + swap(inner_sum, axis, step)
            step *= 2
    pre = apply_call(
        right_kernel,
        "right",
        own_operand,
        left_rows,
        g_pieces,
        firsts,
        panel,
        jax.ShapeDtypeStruct((out_rows, width), f32),
        [turned],
    )
    pre = lax.dynamic_slice_in_dim(pre, fac_index * block_cols, block_cols, 1)
    return pre * (width / jnp.sqrt(inner_sum + epsilon))


def solution(mesh):
    placed = (
        P("dp", None),
        P("dp", "fac"),
        P(),
        P("dp", "fac", None, None),
        P("fac", "dp"),
        P("dp", "fac"),
    )
    return jax.shard_map(
        per_device, mesh=mesh, in_specs=placed, out_specs=P("dp", "fac"), check_vma=False
    )
```

```python
import functools

import jax
import jax.numpy as jnp
from jax import lax
from jax.experimental import pallas as pl
from jax.experimental.pallas import tpu as pltpu
from jax.sharding import PartitionSpec as P

ORBS = 256
NE = 48


damping = 0.1
epsilon = 1e-06
f32 = jnp.float32
bf16 = jnp.bfloat16
contract_first = (((0,), (0,)), ((), ()))


def keep_mask(occupations):
    before = jnp.cumsum(occupations, axis=1) - occupations
    position = lax.broadcasted_iota(jnp.int32, occupations.shape, 1)
    forced = (before == NE) | (position - before == ORBS - NE)
    return 1 - forced.astype(jnp.int32)


def grid_of(count):
    core = 2 if count % 2 == 0 else 1
    chips = count // core
    inner = 1
    while inner * inner * 4 <= chips:
        inner *= 2
    return chips // inner, inner, core


def swap(value, axis, step):
    size = lax.axis_size(axis)
    return lax.ppermute(value, axis, [(i, i ^ step) for i in range(size)])


def collect(value, axis, count, stride):
    return [value] + [swap(value, axis, k * stride) for k in range(1, count)]


def in_order(pieces, own, axis):
    if len(pieces) == 2:
        first, second = pieces
        lower = own == 0
        return jnp.concatenate(
            [jnp.where(lower, first, second), jnp.where(lower, second, first)], axis
        )
    width = pieces[0].shape[axis]
    shape = list(pieces[0].shape)
    shape[axis] = width * len(pieces)
    whole = jnp.zeros(shape, pieces[0].dtype)
    for k, piece in enumerate(pieces):
        whole = lax.dynamic_update_slice_in_dim(whole, piece, (own ^ k) * width, axis)
    return whole


def dot(left, right):
    return jnp.dot(left, right, preferred_element_type=f32)


def kernel_params():
    return pltpu.CompilerParams(vmem_limit_bytes=56 * 1024 * 1024)


def whole():
    return pl.BlockSpec(memory_space=pltpu.VMEM)


def scalars():
    return pl.BlockSpec(memory_space=pltpu.SMEM)


def anywhere():
    return pl.BlockSpec(memory_space=pl.ANY)


def value_kernel(copies_of, halves, index_ref, keep_ref, probs_ref, *refs):
    upstream_refs, refs = refs[:halves], refs[halves:]
    *piece_refs, out_ref, weights, out_grad, sem = refs
    data_index, fac_index = index_ref[0], index_ref[1]
    width = upstream_refs[0].shape[1]
    copies = copies_of(data_index, piece_refs, weights, sem)
    for copy in copies:
        copy.start()
    for copy in copies:
        copy.wait()
    total = None
    for k, ref in enumerate(upstream_refs):
        place = pl.multiple_of((fac_index ^ k) * width, width)
        part = lax.dot_general(
            ref[...],
            weights[:, pl.ds(place, width)],
            (((1,), (1,)), ((), ())),
            preferred_element_type=f32,
        )
        total = part if total is None else total + part
    out_grad[...] = (total * keep_ref[...]).astype(bf16)
    samples, heads, span, _ = probs_ref.shape
    head_width = out_ref.shape[1] // heads
    for s in range(samples):
        for h in range(heads):
            rows, cols = pl.ds(s * span, span), pl.ds(h * head_width, head_width)
            out_ref[rows, cols] = lax.dot_general(
                probs_ref[s, h], out_grad[rows, cols], contract_first, preferred_element_type=f32
            ).astype(bf16)


def window_kernel(count, block, scale, where_ref, *refs):
    *pairs, out_ref, scratch = refs
    lefts, rights = pairs[: len(pairs) // 2], pairs[len(pairs) // 2 :]
    blocks = rights[0].shape[1] // block
    rows_at = pl.multiple_of(where_ref[0], block)
    first = where_ref[1]
    turned = [ref[:, pl.ds(rows_at, block)].T for ref in lefts]
    for n in range(count):
        at = first + n
        at = jnp.where(at >= blocks, at - blocks, at)
        cols = pl.ds(pl.multiple_of(at * block, block), block)
        total = dot(turned[0], rights[0][:, cols])
        for left, right in zip(turned[1:], rights[1:]):
            total = total + dot(left, right[:, cols])
        if scratch.shape[0] == out_ref.shape[0]:
            out_ref[:, n * block : (n + 1) * block] = (total * scale).astype(out_ref.dtype)
        else:
            scratch[:, n * block : (n + 1) * block] = total * scale
    if scratch.shape[0] != out_ref.shape[0]:
        rows = out_ref.shape[0]
        out_ref[...] = scratch[pl.ds(pl.multiple_of(where_ref[2], rows), rows), :].astype(out_ref.dtype)


def window(name, lefts, rights, where, rows, block, count, scale, dtype):
    scratch_rows = block if rows != block else rows
    scratch_cols = count * block if rows != block else 128
    return pl.pallas_call(
        functools.partial(window_kernel, count, block, scale),
        name=name,
        in_specs=[scalars()] + [whole()] * (len(lefts) + len(rights)),
        out_specs=whole(),
        out_shape=jax.ShapeDtypeStruct((rows, count * block), dtype),
        scratch_shapes=[pltpu.VMEM((scratch_rows, scratch_cols), f32)],
        compiler_params=kernel_params(),
    )(where, *lefts, *rights)


def load_factor(own, piece_refs, plan, factor, sem, rows, block):
    copies = []
    for ref, (codes, offset) in zip(piece_refs, plan):
        for n, code in enumerate(codes):
            place = pl.multiple_of((own ^ code) * rows, rows)
            column = pl.multiple_of(lax.div(place, block) * block + offset, 128)
            copies.append(
                pltpu.make_async_copy(
                    ref.at[pl.ds(n * rows, rows)],
                    factor.at[pl.ds(place, rows), pl.ds(column, ref.shape[1])],
                    sem,
                )
            )
    for copy in copies:
        copy.start()
    for copy in copies:
        copy.wait()
    blocks = factor.shape[0] // block
    for i in range(blocks):
        for n in range(1, blocks):
            j = (i + n) % blocks
            here = (slice(i * block, (i + 1) * block), slice(j * block, (j + 1) * block))
            if 2 * n <= blocks:
                if i + n >= blocks:
                    factor[here] = factor[here[0], (i + n) * block : (i + n + 1) * block]
            else:
                across = j + blocks - n
                factor[here] = factor[
                    j * block : (j + 1) * block, across * block : (across + 1) * block
                ].T


def first_steps(panel, factor):
    size = factor.shape[0]
    step = min(256, size)
    total = jnp.zeros((8, size), f32)
    for r in range(0, size, step):
        part = factor[r : r + step, :size].astype(f32)
        total = total + jnp.sum((part * part).reshape(step // 8, 8, size), axis=0)
    alpha = lax.rsqrt(jnp.sum(total, keepdims=True))
    first = 2.0 * alpha * panel - alpha * alpha * dot(panel.astype(bf16), factor[:, :size])
    return alpha, first, dot(first.astype(bf16), factor[:, :size])


def left_kernel(plan, rows, block, own_ref, panel_ref, *refs):
    *piece_refs, out_ref, factor, sem = refs
    load_factor(own_ref[0], piece_refs, plan, factor, sem, rows, block)
    size = factor.shape[0]
    alpha, first, turned = first_steps(panel_ref[...], factor)
    last = dot(turned.astype(bf16), factor[:, :size])
    result = (2.0 * first - 2.0 * alpha * turned + alpha * alpha * last).astype(bf16)
    width = out_ref.shape[2]
    for n in range(out_ref.shape[0]):
        out_ref[n] = result[:, n * width : (n + 1) * width]


def gathered_rows(own, blocks_ref, turned):
    count, rows, _ = blocks_ref.shape
    for n in range(count):
        turned[n * rows : (n + 1) * rows, :] = blocks_ref[own ^ n].astype(f32)
    return turned[: count * rows, :].T


def right_kernel(plan, rows, block, own_ref, blocks_ref, grad_ref, *refs):
    *piece_refs, out_ref, sum_ref, factor, turned_ref, first_ref, second_ref, sem = refs
    own = own_ref[0]
    load_factor(own, piece_refs, plan, factor, sem, rows, block)
    alpha, first, second = first_steps(gathered_rows(own, blocks_ref, turned_ref), factor)
    first_ref[...] = first
    second_ref[...] = second
    width = out_ref.shape[1]
    mine = pl.ds(pl.multiple_of(own_ref[1] * width, width), width)
    last = dot(second.astype(bf16), factor[:, mine])
    result = 2.0 * first_ref[:, mine] - 2.0 * alpha * second_ref[:, mine] + alpha * alpha * last
    out_ref[...] = result
    grad = gathered_rows(own_ref[2], grad_ref, turned_ref)
    sum_ref[...] = jnp.broadcast_to(jnp.sum(grad * result, keepdims=True), sum_ref.shape)


def apply_call(kernel, name, operands, pieces, plan, rows, block, size, out_specs, out_shape, scratch):
    return pl.pallas_call(
        functools.partial(kernel, plan, rows, block),
        name=name,
        in_specs=[scalars()] + [whole()] * (len(operands) - 1) + [anywhere()] * len(pieces),
        out_specs=out_specs,
        out_shape=out_shape,
        scratch_shapes=[pltpu.VMEM((size, size + size // 2), bf16)]
        + scratch
        + [pltpu.SemaphoreType.DMA],
        compiler_params=kernel_params(),
    )(*operands, *pieces)


def per_device(occupations, stream, norm_gain, probs, w_out, cotangent):
    width = norm_gain.shape[0]
    samples = occupations.shape[0]
    tokens = samples * ORBS
    data_count = lax.axis_size("dp")
    fac_count = lax.axis_size("fac")
    outer, inner, cores = grid_of(data_count)
    data_index = lax.axis_index("dp").astype(jnp.int32)
    fac_index = lax.axis_index("fac").astype(jnp.int32)
    core_index = data_index % cores
    inner_index = data_index // cores % inner
    outer_index = data_index // (cores * inner)
    inner_step = cores
    outer_step = cores * inner
    block_cols = width // fac_count
    scale = 1.0 / (tokens * data_count)
    quarter = width // (fac_count * cores)
    slab = quarter // inner
    panel = slab // outer
    block = max(slab, 128)
    own = ((fac_index * cores + core_index) * inner + inner_index) * outer + outer_index

    chunks = 2
    chunk_rows = w_out.shape[0] // chunks
    w_cols = w_out.shape[1]
    cotangents = collect(cotangent, "fac", fac_count, 1)
    pieces = []
    for n in range(chunks):
        part = w_out[n * chunk_rows : (n + 1) * chunk_rows]
        part = jnp.stack(collect(part, "dp", outer, outer_step))
        part = jnp.stack(collect(part, "dp", inner, inner_step))
        pieces += collect(part, "dp", cores, 1)

    def weight_copies(index, piece_refs, weights, sem):
        copies = []
        for n, ref in enumerate(piece_refs):
            rows = pl.ds(n // cores * chunk_rows, chunk_rows)
            for x in range(inner):
                for z in range(outer):
                    place = index ^ ((z * inner + x) * cores + n % cores)
                    columns = pl.ds(pl.multiple_of(place * w_cols, w_cols), w_cols)
                    copies.append(pltpu.make_async_copy(ref.at[x, z], weights.at[rows, columns], sem))
        return copies

    stream_after, _ = lax.optimization_barrier((stream, cotangents[-1]))
    stream_whole = in_order(collect(stream_after, "fac", fac_count, 1), fac_index, 1)
    values = stream_whole.astype(f32)
    mean_square = jnp.mean(values * values, axis=1, keepdims=True)
    normed = (values * lax.rsqrt(mean_square + epsilon) * norm_gain).astype(bf16)
    keep = keep_mask(occupations).reshape(tokens, 1).astype(f32)
    if w_cols % 128 == 0:
        value_local = pl.pallas_call(
            functools.partial(value_kernel, weight_copies, fac_count),
            name="value",
            in_specs=[scalars()] + [whole()] * (2 + fac_count) + [anywhere()] * len(pieces),
            out_specs=whole(),
            out_shape=jax.ShapeDtypeStruct((tokens, block_cols), bf16),
            scratch_shapes=[
                pltpu.VMEM((w_out.shape[0], width), bf16),
                pltpu.VMEM((tokens, block_cols), bf16),
                pltpu.SemaphoreType.DMA,
            ],
            compiler_params=kernel_params(),
        )(jnp.stack([data_index, fac_index]), keep, probs, *cotangents, *pieces)
    else:
        w_whole = jnp.zeros((w_out.shape[0], width), bf16)
        for n, piece in enumerate(pieces):
            for x in range(inner):
                for z in range(outer):
                    place = data_index ^ ((z * inner + x) * cores + n % cores)
                    w_whole = lax.dynamic_update_slice(
                        w_whole, piece[x, z], (n // cores * chunk_rows, place * w_cols)
                    )
        out_grad = lax.dot_general(
            in_order(cotangents, fac_index, 1) * keep.astype(bf16),
            w_whole,
            (((1,), (1,)), ((), ())),
            preferred_element_type=f32,
        ).astype(bf16)
        per_head = out_grad.reshape(samples, ORBS, probs.shape[1], -1)
        value_local = jnp.einsum("shij,sihe->sjhe", probs, per_head, preferred_element_type=f32)
        value_local = value_local.reshape(tokens, block_cols).astype(bf16)

    value_whole = in_order(collect(value_local, "fac", fac_count, 1), fac_index, 1)
    normeds = collect(normed, "dp", cores, 1)
    values_both = collect(value_whole, "dp", cores, 1)
    normeds_after, _ = lax.optimization_barrier((normeds, value_local))

    first_row = (fac_index * cores + core_index) * quarter

    def summed(name, lefts, rights, symmetric):
        count = width // 2 // block + 1 if symmetric else width // block
        operands = () if symmetric else rights
        parts = []
        for k in list(range(1, inner)) + [0]:
            row = first_row + (inner_index ^ k) * slab
            at = row // block
            where = jnp.stack([at * block, at if symmetric else jnp.int32(0), row - at * block])
            parts.append(
                window(
                    f"{name}_{k}",
                    lefts,
                    lefts if symmetric else operands,
                    where,
                    slab,
                    block,
                    count,
                    scale,
                    bf16 if k else f32,
                )
            )
        total = parts[-1]
        for k in range(1, inner):
            total = total + swap(parts[k - 1], "dp", k * inner_step).astype(f32)
        total = total.reshape(outer, panel, count * block)
        pieces = [
            lax.dynamic_index_in_dim(total, outer_index ^ k, 0, keepdims=False) for k in range(outer)
        ]
        result = pieces[0]
        for k in range(1, outer):
            result = result + swap(pieces[k].astype(bf16), "dp", k * outer_step).astype(f32)
        return result

    window_cols = width // 2 + block
    row_ids = own * panel + lax.broadcasted_iota(jnp.int32, (panel, window_cols), 0)
    col_ids = own * panel // block * block + lax.broadcasted_iota(
        jnp.int32, (panel, window_cols), 1
    )
    damp = damping * (row_ids == col_ids).astype(f32)
    splits = (0, window_cols // 256 * 128, window_cols)

    def panels_of(result):
        panels = collect((result + damp).astype(bf16), "dp", outer, outer_step)
        steps = [
            ("dp", inner, inner_step, outer),
            ("fac", fac_count, 1, outer * inner * cores),
        ]
        pieces, plan = [], []
        for n, order in enumerate((steps, steps[::-1])):
            parts = [piece[:, splits[n] : splits[n + 1]] for piece in panels]
            codes = list(range(outer))
            for axis, size, stride, code_step in order:
                parts = collect(jnp.concatenate(parts, axis=0), axis, size, stride)
                codes = [code + code_step * k for k in range(size) for code in codes]
            parts = collect(jnp.concatenate(parts, axis=0), "dp", cores, 1)
            for k, part in enumerate(parts):
                pieces.append(part)
                plan.append(([code + outer * inner * k for code in codes], splits[n]))
        return pieces, plan

    a_pieces, plan = panels_of(summed("stream_factor", normeds_after, None, True))
    g_pieces, _ = panels_of(summed("value_factor", values_both, None, True))
    grad_cols = summed("grad", values_both, normeds, False)

    out_rows = width // data_count

    def exchange(blocks):
        blocks = blocks.reshape(outer, inner, cores, panel, out_rows)
        at = lambda part, index, axis: lax.dynamic_index_in_dim(part, index, axis, keepdims=False)
        blocks = jnp.stack(
            [at(blocks, core_index, 2)]
            + [swap(at(blocks, core_index ^ k, 2), "dp", k) for k in range(1, cores)]
        )
        blocks = jnp.stack(
            [at(blocks, inner_index, 2)]
            + [swap(at(blocks, inner_index ^ k, 2), "dp", k * inner_step) for k in range(1, inner)],
            axis=1,
        )
        blocks = jnp.stack(
            [at(blocks, outer_index, 2)]
            + [swap(at(blocks, outer_index ^ k, 2), "dp", k * outer_step) for k in range(1, outer)],
            axis=2,
        )
        return blocks.reshape(cores * inner * outer, panel, out_rows)

    grad_blocks = jnp.transpose(
        grad_cols.astype(bf16).reshape(panel, data_count, out_rows), (1, 0, 2)
    )
    grad_rows = exchange(grad_blocks)
    left = apply_call(
        left_kernel,
        "left",
        (own.reshape(1), grad_cols),
        a_pieces,
        plan,
        panel,
        block,
        width,
        whole(),
        jax.ShapeDtypeStruct((data_count, panel, out_rows), bf16),
        [],
    )
    left_rows = jnp.concatenate(collect(exchange(left), "fac", fac_count, 1), axis=0)
    pre, inner_sum = apply_call(
        right_kernel,
        "right",
        (jnp.stack([own, fac_index, own % data_count]), left_rows, grad_rows),
        g_pieces,
        plan,
        panel,
        block,
        width,
        (whole(), whole()),
        (
            jax.ShapeDtypeStruct((out_rows, block_cols), f32),
            jax.ShapeDtypeStruct((1, 128), f32),
        ),
        [
            pltpu.VMEM((width, out_rows), f32),
            pltpu.VMEM((out_rows, width), f32),
            pltpu.VMEM((out_rows, width), f32),
        ],
    )
    for axis, size in (("fac", fac_count), ("dp", data_count)):
        step = 1
        while step < size:
            inner_sum = inner_sum + swap(inner_sum, axis, step)
            step *= 2
    return pre * (width / jnp.sqrt(inner_sum[:, :1] + epsilon))


def solution(mesh):
    placed = (
        P("dp", None),
        P("dp", "fac"),
        P(),
        P("dp", "fac", None, None),
        P("fac", "dp"),
        P("dp", "fac"),
    )
    return jax.shard_map(
        per_device, mesh=mesh, in_specs=placed, out_specs=P("dp", "fac"), check_vma=False
    )
```

```python
import functools

import jax
import jax.numpy as jnp
from jax import lax
from jax.experimental import pallas as pl
from jax.experimental.pallas import tpu as pltpu
from jax.sharding import PartitionSpec as P

ORBS = 256
NE = 48


damping = 0.1
epsilon = 1e-06
f32 = jnp.float32
bf16 = jnp.bfloat16
contract_first = (((0,), (0,)), ((), ()))


def keep_mask(occupations):
    before = jnp.cumsum(occupations, axis=1) - occupations
    position = lax.broadcasted_iota(jnp.int32, occupations.shape, 1)
    forced = (before == NE) | (position - before == ORBS - NE)
    return 1 - forced.astype(jnp.int32)


def grid_of(count):
    core = 2 if count % 2 == 0 else 1
    chips = count // core
    inner = 1
    while inner * inner * 4 <= chips:
        inner *= 2
    return chips // inner, inner, core


def swap(value, axis, step):
    size = lax.axis_size(axis)
    return lax.ppermute(value, axis, [(i, i ^ step) for i in range(size)])


def collect(value, axis, count, stride):
    return [value] + [swap(value, axis, k * stride) for k in range(1, count)]


def in_order(pieces, own, axis):
    if len(pieces) == 2:
        first, second = pieces
        lower = own == 0
        return jnp.concatenate(
            [jnp.where(lower, first, second), jnp.where(lower, second, first)], axis
        )
    width = pieces[0].shape[axis]
    shape = list(pieces[0].shape)
    shape[axis] = width * len(pieces)
    whole = jnp.zeros(shape, pieces[0].dtype)
    for k, piece in enumerate(pieces):
        whole = lax.dynamic_update_slice_in_dim(whole, piece, (own ^ k) * width, axis)
    return whole


def dot(left, right):
    return jnp.dot(left, right, preferred_element_type=f32)


def kernel_params():
    return pltpu.CompilerParams(vmem_limit_bytes=56 * 1024 * 1024)


def whole():
    return pl.BlockSpec(memory_space=pltpu.VMEM)


def scalars():
    return pl.BlockSpec(memory_space=pltpu.SMEM)


def anywhere():
    return pl.BlockSpec(memory_space=pl.ANY)


def value_kernel(copies_of, halves, index_ref, keep_ref, probs_ref, *refs):
    upstream_refs, refs = refs[:halves], refs[halves:]
    *piece_refs, out_ref, weights, out_grad, sem = refs
    data_index, fac_index = index_ref[0], index_ref[1]
    width = upstream_refs[0].shape[1]
    copies = copies_of(data_index, piece_refs, weights, sem)
    for copy in copies:
        copy.start()
    for copy in copies:
        copy.wait()
    total = None
    for k, ref in enumerate(upstream_refs):
        place = pl.multiple_of((fac_index ^ k) * width, width)
        part = lax.dot_general(
            ref[...],
            weights[:, pl.ds(place, width)],
            (((1,), (1,)), ((), ())),
            preferred_element_type=f32,
        )
        total = part if total is None else total + part
    out_grad[...] = (total * keep_ref[...]).astype(bf16)
    samples, heads, span, _ = probs_ref.shape
    head_width = out_ref.shape[1] // heads
    for s in range(samples):
        for h in range(heads):
            rows, cols = pl.ds(s * span, span), pl.ds(h * head_width, head_width)
            out_ref[rows, cols] = lax.dot_general(
                probs_ref[s, h], out_grad[rows, cols], contract_first, preferred_element_type=f32
            ).astype(bf16)


def window_kernel(count, block, scale, halves, where_ref, *refs):
    *pairs, out_ref, lefts, rights, scratch, left_sem, right_sems = refs
    pieces = len(pairs) // (1 + halves)
    left_refs, right_refs = pairs[:pieces], pairs[pieces:]
    half_blocks = right_refs[0].shape[1] // block
    blocks = half_blocks * halves
    rows_at = pl.multiple_of(where_ref[0], block)
    first, own_half = where_ref[1], where_ref[3]
    left_copies = [
        pltpu.make_async_copy(ref.at[:, pl.ds(rows_at, block)], lefts.at[t], left_sem)
        for t, ref in enumerate(left_refs)
    ]
    for copy in left_copies:
        copy.start()

    def right_copy(t, k, n, at):
        cols = pl.ds(pl.multiple_of(lax.rem(at, half_blocks) * block, block), block)
        return pltpu.make_async_copy(
            right_refs[t * halves + k].at[:, cols], rights.at[n, t], right_sems.at[n]
        )

    for n in range(count):
        at = lax.rem(first + n, blocks)
        for t in range(pieces):
            for k in range(halves):

                @pl.when((lax.div(at, half_blocks) ^ own_half) == k)
                def _():
                    right_copy(t, k, n, at).start()

    for copy in left_copies:
        copy.wait()
    turned = [lefts[t].T for t in range(pieces)]
    direct = scratch.shape[0] != block
    for n in range(count):
        for t in range(pieces):
            right_copy(t, 0, n, first).wait()
        total = dot(turned[0], rights[n, 0])
        for t in range(1, pieces):
            total = total + dot(turned[t], rights[n, t])
        cols = slice(n * block, (n + 1) * block)
        if direct:
            out_ref[:, cols] = (total * scale).astype(out_ref.dtype)
        else:
            scratch[:, cols] = total * scale
    if not direct:
        rows = out_ref.shape[0]
        out_ref[...] = scratch[pl.ds(pl.multiple_of(where_ref[2], rows), rows), :].astype(out_ref.dtype)


def window(name, lefts, rights, where, rows, block, count, scale, dtype):
    pieces, halves = len(rights), len(rights[0])
    tokens = lefts[0].shape[0]
    direct = rows == block
    return pl.pallas_call(
        functools.partial(window_kernel, count, block, scale, halves),
        name=name,
        in_specs=[scalars()] + [anywhere()] * (pieces * (1 + halves)),
        out_specs=whole(),
        out_shape=jax.ShapeDtypeStruct((rows, count * block), dtype),
        scratch_shapes=[
            pltpu.VMEM((pieces, tokens, block), bf16),
            pltpu.VMEM((count, pieces, tokens, block), bf16),
            pltpu.VMEM((8, 128) if direct else (block, count * block), f32),
            pltpu.SemaphoreType.DMA,
            pltpu.SemaphoreType.DMA((count,)),
        ],
        compiler_params=kernel_params(),
    )(where, *lefts, *(half for piece in rights for half in piece))


def load_factor(own, piece_refs, plan, factor, sem, rows, block):
    copies = []
    for ref, (codes, offset) in zip(piece_refs, plan):
        for n, code in enumerate(codes):
            place = pl.multiple_of((own ^ code) * rows, rows)
            column = pl.multiple_of(lax.div(place, block) * block + offset, 128)
            copies.append(
                pltpu.make_async_copy(
                    ref.at[pl.ds(n * rows, rows)],
                    factor.at[pl.ds(place, rows), pl.ds(column, ref.shape[1])],
                    sem,
                )
            )
    for copy in copies:
        copy.start()
    for copy in copies:
        copy.wait()
    blocks = factor.shape[0] // block
    for i in range(blocks):
        for n in range(1, blocks):
            j = (i + n) % blocks
            here = (slice(i * block, (i + 1) * block), slice(j * block, (j + 1) * block))
            if 2 * n <= blocks:
                if i + n >= blocks:
                    factor[here] = factor[here[0], (i + n) * block : (i + n + 1) * block]
            else:
                across = j + blocks - n
                factor[here] = factor[
                    j * block : (j + 1) * block, across * block : (across + 1) * block
                ].T


def first_steps(panel, factor):
    size = factor.shape[0]
    step = min(256, size)
    total = jnp.zeros((8, size), f32)
    for r in range(0, size, step):
        part = factor[r : r + step, :size].astype(f32)
        total = total + jnp.sum((part * part).reshape(step // 8, 8, size), axis=0)
    alpha = lax.rsqrt(jnp.sum(total, keepdims=True))
    first = 2.0 * alpha * panel - alpha * alpha * dot(panel.astype(bf16), factor[:, :size])
    return alpha, first, dot(first.astype(bf16), factor[:, :size])


def left_kernel(plan, rows, block, own_ref, panel_ref, *refs):
    *piece_refs, out_ref, factor, sem = refs
    load_factor(own_ref[0], piece_refs, plan, factor, sem, rows, block)
    size = factor.shape[0]
    alpha, first, turned = first_steps(panel_ref[...], factor)
    last = dot(turned.astype(bf16), factor[:, :size])
    result = (2.0 * first - 2.0 * alpha * turned + alpha * alpha * last).astype(bf16)
    width = out_ref.shape[2]
    for n in range(out_ref.shape[0]):
        out_ref[n] = result[:, n * width : (n + 1) * width]


def gathered_rows(own, blocks_ref, turned):
    count, rows, _ = blocks_ref.shape
    for n in range(count):
        turned[n * rows : (n + 1) * rows, :] = blocks_ref[own ^ n].astype(f32)
    return turned[: count * rows, :].T


def right_kernel(plan, rows, block, own_ref, blocks_ref, grad_ref, *refs):
    *piece_refs, out_ref, sum_ref, factor, turned_ref, first_ref, second_ref, sem = refs
    own = own_ref[0]
    load_factor(own, piece_refs, plan, factor, sem, rows, block)
    alpha, first, second = first_steps(gathered_rows(own, blocks_ref, turned_ref), factor)
    first_ref[...] = first
    second_ref[...] = second
    width = out_ref.shape[1]
    mine = pl.ds(pl.multiple_of(own_ref[1] * width, width), width)
    last = dot(second.astype(bf16), factor[:, mine])
    result = 2.0 * first_ref[:, mine] - 2.0 * alpha * second_ref[:, mine] + alpha * alpha * last
    out_ref[...] = result
    grad = gathered_rows(own_ref[2], grad_ref, turned_ref)
    sum_ref[...] = jnp.broadcast_to(jnp.sum(grad * result, keepdims=True), sum_ref.shape)


def apply_call(kernel, name, operands, pieces, plan, rows, block, size, out_specs, out_shape, scratch):
    return pl.pallas_call(
        functools.partial(kernel, plan, rows, block),
        name=name,
        in_specs=[scalars()] + [whole()] * (len(operands) - 1) + [anywhere()] * len(pieces),
        out_specs=out_specs,
        out_shape=out_shape,
        scratch_shapes=[pltpu.VMEM((size, size + size // 2), bf16)]
        + scratch
        + [pltpu.SemaphoreType.DMA],
        compiler_params=kernel_params(),
    )(*operands, *pieces)


def per_device(occupations, stream, norm_gain, probs, w_out, cotangent):
    width = norm_gain.shape[0]
    samples = occupations.shape[0]
    tokens = samples * ORBS
    data_count = lax.axis_size("dp")
    fac_count = lax.axis_size("fac")
    outer, inner, cores = grid_of(data_count)
    data_index = lax.axis_index("dp").astype(jnp.int32)
    fac_index = lax.axis_index("fac").astype(jnp.int32)
    core_index = data_index % cores
    inner_index = data_index // cores % inner
    outer_index = data_index // (cores * inner)
    inner_step = cores
    outer_step = cores * inner
    block_cols = width // fac_count
    scale = 1.0 / (tokens * data_count)
    quarter = width // (fac_count * cores)
    slab = quarter // inner
    panel = slab // outer
    block = max(slab, 128)
    own = ((fac_index * cores + core_index) * inner + inner_index) * outer + outer_index

    chunks = 2
    chunk_rows = w_out.shape[0] // chunks
    w_cols = w_out.shape[1]
    pieces = []
    last = None
    for n in range(chunks):
        part = w_out[n * chunk_rows : (n + 1) * chunk_rows]
        if last is not None:
            part, _ = lax.optimization_barrier((part, last))
        part = collect(part, "dp", outer, outer_step)
        last = part[-1]
        part = jnp.stack(part)
        part = jnp.stack(collect(part, "dp", inner, inner_step))
        pieces += collect(part, "dp", cores, 1)

    def weight_copies(index, piece_refs, weights, sem):
        copies = []
        for n, ref in enumerate(piece_refs):
            rows = pl.ds(n // cores * chunk_rows, chunk_rows)
            for x in range(inner):
                for z in range(outer):
                    place = index ^ ((z * inner + x) * cores + n % cores)
                    columns = pl.ds(pl.multiple_of(place * w_cols, w_cols), w_cols)
                    copies.append(pltpu.make_async_copy(ref.at[x, z], weights.at[rows, columns], sem))
        return copies

    streams = collect(stream, "fac", fac_count, 1)
    cotangent_after, _ = lax.optimization_barrier((cotangent, streams[-1]))
    cotangents = collect(cotangent_after, "fac", fac_count, 1)
    stream_whole = in_order(streams, fac_index, 1)
    values = stream_whole.astype(f32)
    mean_square = jnp.mean(values * values, axis=1, keepdims=True)
    normed = (values * lax.rsqrt(mean_square + epsilon) * norm_gain).astype(bf16)
    keep = keep_mask(occupations).reshape(tokens, 1).astype(f32)
    if w_cols % 128 == 0:
        value_local = pl.pallas_call(
            functools.partial(value_kernel, weight_copies, fac_count),
            name="value",
            in_specs=[scalars()] + [whole()] * (2 + fac_count) + [anywhere()] * len(pieces),
            out_specs=whole(),
            out_shape=jax.ShapeDtypeStruct((tokens, block_cols), bf16),
            scratch_shapes=[
                pltpu.VMEM((w_out.shape[0], width), bf16),
                pltpu.VMEM((tokens, block_cols), bf16),
                pltpu.SemaphoreType.DMA,
            ],
            compiler_params=kernel_params(),
        )(jnp.stack([data_index, fac_index]), keep, probs, *cotangents, *pieces)
    else:
        w_whole = jnp.zeros((w_out.shape[0], width), bf16)
        for n, piece in enumerate(pieces):
            for x in range(inner):
                for z in range(outer):
                    place = data_index ^ ((z * inner + x) * cores + n % cores)
                    w_whole = lax.dynamic_update_slice(
                        w_whole, piece[x, z], (n // cores * chunk_rows, place * w_cols)
                    )
        out_grad = lax.dot_general(
            in_order(cotangents, fac_index, 1) * keep.astype(bf16),
            w_whole,
            (((1,), (1,)), ((), ())),
            preferred_element_type=f32,
        ).astype(bf16)
        per_head = out_grad.reshape(samples, ORBS, probs.shape[1], -1)
        value_local = jnp.einsum("shij,sihe->sjhe", probs, per_head, preferred_element_type=f32)
        value_local = value_local.reshape(tokens, block_cols).astype(bf16)

    normeds = [[piece] for piece in collect(normed, "dp", cores, 1)]
    value_halves = [
        collect(half, "dp", cores, 1) for half in collect(value_local, "fac", fac_count, 1)
    ]
    values_both = [list(pieces) for pieces in zip(*value_halves)]
    quarter_row = core_index * quarter
    first_row = fac_index * block_cols + quarter_row

    def summed(name, lefts, left_row, rights, symmetric):
        count = width // 2 // block + 1 if symmetric else width // block
        parts = []
        for k in list(range(1, inner)) + [0]:
            shift = (inner_index ^ k) * slab
            left = left_row + shift
            at = (first_row + shift) // block
            where = jnp.stack(
                [
                    left // block * block,
                    at if symmetric else jnp.int32(0),
                    left - left // block * block,
                    fac_index if len(rights[0]) > 1 else jnp.int32(0),
                ]
            )
            parts.append(
                window(
                    f"{name}_{k}", lefts, rights, where, slab, block, count, scale, bf16 if k else f32
                )
            )
        total = parts[-1]
        for k in range(1, inner):
            total = total + swap(parts[k - 1], "dp", k * inner_step).astype(f32)
        total = total.reshape(outer, panel, count * block)
        pieces = [
            lax.dynamic_index_in_dim(total, outer_index ^ k, 0, keepdims=False) for k in range(outer)
        ]
        result = pieces[0]
        for k in range(1, outer):
            result = result + swap(pieces[k].astype(bf16), "dp", k * outer_step).astype(f32)
        return result

    window_cols = width // 2 + block
    row_ids = own * panel + lax.broadcasted_iota(jnp.int32, (panel, window_cols), 0)
    col_ids = own * panel // block * block + lax.broadcasted_iota(
        jnp.int32, (panel, window_cols), 1
    )
    damp = damping * (row_ids == col_ids).astype(f32)
    splits = (0, window_cols // 256 * 128, window_cols)

    def panels_of(result):
        panels = collect((result + damp).astype(bf16), "dp", outer, outer_step)
        steps = [
            ("dp", inner, inner_step, outer),
            ("fac", fac_count, 1, outer * inner * cores),
        ]
        pieces, plan = [], []
        for n, order in enumerate((steps, steps[::-1])):
            parts = [piece[:, splits[n] : splits[n + 1]] for piece in panels]
            codes = list(range(outer))
            for axis, size, stride, code_step in order:
                parts = collect(jnp.concatenate(parts, axis=0), axis, size, stride)
                codes = [code + code_step * k for k in range(size) for code in codes]
            parts = collect(jnp.concatenate(parts, axis=0), "dp", cores, 1)
            for k, part in enumerate(parts):
                pieces.append(part)
                plan.append(([code + outer * inner * k for code in codes], splits[n]))
        return pieces, plan

    stream_lefts = [piece[0] for piece in normeds]
    value_lefts = [piece[0] for piece in values_both]
    a_pieces, plan = panels_of(summed("stream_factor", stream_lefts, first_row, normeds, True))
    grad_cols = summed("grad", value_lefts, quarter_row, normeds, False)
    g_pieces, _ = panels_of(summed("value_factor", value_lefts, quarter_row, values_both, True))

    out_rows = width // data_count

    def exchange(blocks):
        blocks = blocks.reshape(outer, inner, cores, panel, out_rows)
        at = lambda part, index, axis: lax.dynamic_index_in_dim(part, index, axis, keepdims=False)
        blocks = jnp.stack(
            [at(blocks, core_index, 2)]
            + [swap(at(blocks, core_index ^ k, 2), "dp", k) for k in range(1, cores)]
        )
        blocks = jnp.stack(
            [at(blocks, inner_index, 2)]
            + [swap(at(blocks, inner_index ^ k, 2), "dp", k * inner_step) for k in range(1, inner)],
            axis=1,
        )
        blocks = jnp.stack(
            [at(blocks, outer_index, 2)]
            + [swap(at(blocks, outer_index ^ k, 2), "dp", k * outer_step) for k in range(1, outer)],
            axis=2,
        )
        return blocks.reshape(cores * inner * outer, panel, out_rows)

    grad_blocks = jnp.transpose(
        grad_cols.astype(bf16).reshape(panel, data_count, out_rows), (1, 0, 2)
    )
    grad_rows = exchange(grad_blocks)
    left = apply_call(
        left_kernel,
        "left",
        (own.reshape(1), grad_cols),
        a_pieces,
        plan,
        panel,
        block,
        width,
        whole(),
        jax.ShapeDtypeStruct((data_count, panel, out_rows), bf16),
        [],
    )
    left_rows = jnp.concatenate(collect(exchange(left), "fac", fac_count, 1), axis=0)
    pre, inner_sum = apply_call(
        right_kernel,
        "right",
        (jnp.stack([own, fac_index, own % data_count]), left_rows, grad_rows),
        g_pieces,
        plan,
        panel,
        block,
        width,
        (whole(), whole()),
        (
            jax.ShapeDtypeStruct((out_rows, block_cols), f32),
            jax.ShapeDtypeStruct((1, 128), f32),
        ),
        [
            pltpu.VMEM((width, out_rows), f32),
            pltpu.VMEM((out_rows, width), f32),
            pltpu.VMEM((out_rows, width), f32),
        ],
    )
    for axis, size in (("fac", fac_count), ("dp", data_count)):
        step = 1
        while step < size:
            inner_sum = inner_sum + swap(inner_sum, axis, step)
            step *= 2
    return pre * (width / jnp.sqrt(inner_sum[:, :1] + epsilon))


def solution(mesh):
    placed = (
        P("dp", None),
        P("dp", "fac"),
        P(),
        P("dp", "fac", None, None),
        P("fac", "dp"),
        P("dp", "fac"),
    )
    return jax.shard_map(
        per_device, mesh=mesh, in_specs=placed, out_specs=P("dp", "fac"), check_vma=False
    )
```
